128 devices in a mesh: sess: 16 (over z, x), act: 8 (over y, core).
Axes of the slice: x: 4, y: 4, z: 4, core: 2. Of those that a mesh axis runs over, the one named last changes fastest.
Arguments:
- hist: bfloat16 [8192, 131072], P('sess', 'act'), may hold values from 0.049804688 to 5
- tile_mask: int32 [64, 1024], P('sess', 'act'), may hold values 0 or 1
- planes: bfloat16 [131072, 1024], P('act', 'sess'), may hold values from -0.015625 to 0.015625
- pairs: int32 [256, 2], P('sess'), may hold values from 0 to 63
Outputs:
- scores: float32 [256, 128, 128], P(('sess', 'act'))
The draws below stay inside these ranges and needn't reach their ends.
All inputs are finite; a program needn't handle non-finite values. No bound on the sum of `tile_mask` on one device may be relied on, other than what follows from the above.
Results may differ from the reference program's by a relative error of at most 0.0003.
Values may be sent and summed in bfloat16 or wider, within the bound.
A program may use at most 192 MiB of HBM per device.

```python
import math
import jax
import jax.numpy as jnp
from jax import lax

A = 131072
P_SIZE = 1024
BLK = 128
SESSIONS = 8192
NB = 64
NPAIR = 256


def set_ends(result, rng, least, high):
    extent = result.shape
    spot = [jax.random.randint(jax.random.fold_in(rng, axis), (), 0, extent[axis]) for axis in range(len(extent))]
    result = result.at[tuple(spot)].set(least)
    longest = extent.index(max(extent))
    spot[longest] = (spot[longest] + 1) % extent[longest]
    return result.at[tuple(spot)].set(high)


def block_scale(own_key, extent, split, low, high):
    level = 1.0
    for dim, shards_of in split:
        heights = jax.random.uniform(jax.random.fold_in(jax.random.fold_in(own_key, 6), dim), (shards_of,), jnp.float32, low / len(split), high / len(split))
        level = level * jnp.repeat(jnp.exp(heights), extent[dim] // shards_of).reshape((-1,) + (1,) * (len(extent) - 1 - dim))
    return level


def centred(rng, extent, spread, limit, split=(), held_as=jnp.bfloat16):
    result = jax.random.normal(rng, extent, jnp.float32) * spread
    if len(split) > 0:
        result = block_scale(rng, extent, split, -0.22, 0.18) * result
    return jnp.clip(result, min=-limit, max=limit).astype(held_as)


def setup_inputs(seed: int = 0) -> dict:
    splits = jax.random.split(jax.random.key(seed), 5)
    hist = jnp.clip(jnp.exp(math.log(5.0) - 4.609084 * jax.random.uniform(splits[0], (SESSIONS, A), jnp.float32) ** block_scale(splits[0], (SESSIONS, A), ((0, 16), (1, 8)), -0.2, 0.2)), 0.049804688, 5.0).astype(jnp.bfloat16)
    tile_mask = set_ends((jax.random.randint(splits[1], (NB, A // BLK), 0, 2) < 1).astype(jnp.int32), jax.random.fold_in(splits[1], 1), 0, 1)
    planes = centred(splits[2], (A, P_SIZE), A ** -0.5, 0.015625, ((0, 8), (1, 16)))
    pairs = set_ends(jax.random.randint(splits[3], (NPAIR, 2), 0, NB), jax.random.fold_in(splits[3], 1), 0, NB - 1).astype(jnp.int32)
    return dict(hist=hist, tile_mask=tile_mask, planes=planes, pairs=pairs)


def reference(hist, tile_mask, planes, pairs):
    nb = tile_mask.shape[0]
    ab = tile_mask.shape[1]
    shaped = hist.reshape(nb, BLK, ab, BLK)
    masked = (shaped * tile_mask.astype(jnp.bfloat16)[:, None, :, None]).reshape(hist.shape)
    wide = jnp.dot(masked, planes, preferred_element_type=jnp.float32)
    sq = lax.optimization_barrier(jnp.sum(wide * wide, axis=1))
    blocks = wide.reshape(nb, BLK, P_SIZE)
    norms = sq.reshape(nb, BLK)

    def one_pair(pair):
        left = blocks[pair[0]]
        right = blocks[pair[1]]
        dots = jnp.dot(left, right.T, precision=lax.Precision.HIGHEST)
        lscale = lax.rsqrt(norms[pair[0]] / P_SIZE + 1e-06)
        rscale = lax.rsqrt(norms[pair[1]] / P_SIZE + 1e-06)
        return dots / P_SIZE * lscale[:, None] * rscale[None, :]
    return lax.map(one_pair, pairs)
```

```python
import heapq

import jax
import jax.numpy as jnp
from jax import lax
from jax.experimental import pallas as pl
from jax.experimental.pallas import tpu as pltpu
from jax.sharding import PartitionSpec as P

MESH = pl.DeviceIdType.MESH
P_SIZE = 1024
RING = 4
UNITS = 4
BLK = 128
KC = 2048


def plan(units, depth, length, latency):
    todo = []
    for u in range(units):
        for s in (1, -1):
            for hop in (1, 2):
                todo.append((u, 0, 0, s, hop))
                todo += [(u, 1, dp, s, hop) for dp in (0, -1, 1, 2)]

    def needs(c):
        u, stage, dp, s, hop = c
        if hop == 2:
            return [(u, stage, dp, s, 1)]
        if stage == 0 or dp == 0:
            return []
        if dp == 2:
            return [(u, 0, 0, 1, 2), (u, 0, 0, -1, 2)]
        return [(u, 0, 0, -dp, 1)]

    def rank(c):
        u, stage, dp, s, hop = c
        far = {2: 2, -1: 1, 1: 1, 0: 0}[dp]
        return (u // 2, stage, hop if stage == 0 else 0, far, hop, u, s)

    todo.sort(key=rank)
    done, events, flying, free, count = set(), [], {}, {}, 0

    def start(now):
        nonlocal count
        out = []
        for c in todo:
            if not all(d in done for d in needs(c)):
                continue
            link = ((c[0] + c[1]) % 2, c[3])
            flying[link] = [f for f in flying.get(link, []) if f > now]
            if len(flying[link]) >= depth:
                continue
            end = max(now, free.get(link, 0.0)) + length / c[4]
            free[link] = end
            flying[link].append(end)
            heapq.heappush(events, (end + latency, count, c))
            count += 1
            out.append(c)
        for c in out:
            todo.remove(c)
        return out

    order = [(None, start(0.0))]
    while events:
        now, _, c = heapq.heappop(events)
        done.add(c)
        order.append((c, start(now)))
    assert not todo
    return order


GATHER = plan(UNITS, 3, 11.3, 2.0)
SPREAD = plan(2, 20, 1.4, 2.0)


def numbered(order):
    ids = {}
    for _, started in order:
        for c in started:
            ids[c] = len(ids)
    return ids


GATHER_IDS = numbered(GATHER)
SPREAD_IDS = numbered(SPREAD)


def arrivals(c):
    u, stage, dp, s, hop = c
    back = -s if hop == 1 else 2
    return (u, back, 0) if stage == 0 else (u, dp, back)


def kernel(
    planes, hist, mask, pairs, out,
    g_ref, h_ref, acc, r1, r2, pb, d_ref, e1, e2,
    own_sem, hist_sem, send, recv, s1, v1, s2, v2, s3, v3, ts, tv, us, uv,
):
    depth = planes.shape[1]
    half = depth // 2
    cols = planes.shape[0] // UNITS
    me = lax.axis_index("sess")
    z, x = me // RING, me % RING
    act = lax.axis_index("act")
    y, core = act // 2, act % 2
    place = (z, x)

    def wrap(v, d):
        return lax.rem(v + d + RING, RING)

    def near(axis, d):
        return {"sess": wrap(z, d) * RING + x if axis == 0 else z * RING + wrap(x, d)}

    def along_y(d):
        return {"act": wrap(y, d) * 2 + core}

    twin = {"act": y * 2 + 1 - core}

    def remote(src, dst, send_sem, recv_sem, device):
        return pltpu.make_async_remote_copy(
            src_ref=src, dst_ref=dst, send_sem=send_sem, recv_sem=recv_sem,
            device_id=device, device_id_type=MESH,
        )

    peers = [near(a, d) for a in (0, 1) for d in (1, -1)]
    peers += [along_y(d) for d in (1, -1, 2)] + [twin]
    barrier = pltpu.get_barrier_semaphore()
    for peer in peers:
        pl.semaphore_signal(barrier, inc=1, device_id=peer, device_id_type=MESH)

    owns = []
    for u in range(UNITS):
        pc, qc = place[u % 2], place[1 - u % 2]
        own = pltpu.make_async_copy(
            planes.at[pl.ds(u * cols, cols)], g_ref.at[u, qc * RING + pc], own_sem.at[u]
        )
        own.start()
        owns.append(own)
    load = pltpu.make_async_copy(hist, h_ref, hist_sem)
    load.start()
    pl.semaphore_wait(barrier, len(peers))
    for own in owns:
        own.wait()

    def ends(c):
        u, stage, dp, s, hop = c
        pc, qc = place[u % 2], place[1 - u % 2]
        axis = (u + stage) % 2
        if stage == 0:
            return pc if hop == 1 else wrap(pc, -s), qc, near(axis, s)
        return wrap(pc, dp), qc if hop == 1 else wrap(qc, -s), near(axis, s)

    def gather_copy(c):
        p, q, device = ends(c)
        ref = g_ref.at[c[0], q * RING + p]
        if c[4] == 2:
            ref = ref.at[:, pl.ds(0 if c[3] == 1 else half, half)]
        i = GATHER_IDS[c]
        return remote(ref, ref, send.at[i], recv.at[i], device)

    def spread_copy(h, c):
        p, q, device = ends(c)
        at = (p * RING + q if c[0] == 0 else q * RING + p) * RING
        if c[4] == 2:
            rows = pl.ds(at if c[3] == 1 else at + 2, 2)
        else:
            rows = pl.ds(at, 4)
        ref = pb.at[rows, pl.ds((2 * h + c[0]) * 32, 32)]
        i = SPREAD_IDS[c]
        return remote(ref, ref, ts.at[h, i], tv.at[h, i], device)

    def batch(u, dq):
        q = wrap(place[1 - u % 2], dq)

        def step(i, total):
            at = pl.ds(pl.multiple_of(i * KC, KC), KC)
            some = g_ref[u, pl.ds(q * RING, RING), :, at].reshape(RING * cols, KC)
            return total + lax.dot_general(
                some, h_ref[:, at], (((1,), (1,)), ((), ())),
                preferred_element_type=jnp.float32,
            )

        rows = h_ref.shape[0]
        total = lax.fori_loop(0, depth // KC, step, jnp.zeros((RING * cols, rows), jnp.float32))
        acc[u, q // 2, pl.ds((q % 2) * 2, 2)] = total.reshape(2, 2 * cols, rows)

    def pair_copy(u):
        return remote(acc.at[u, 1 - core], r1.at[u], s1.at[u], v1.at[u], twin)

    def ring_copy(u, d):
        i = {1: 0, -1: 1, 2: 2}[d]
        return remote(acc.at[u, core, wrap(y, d)], r2.at[u, i], s2.at[u, i], v2.at[u, i], along_y(d))

    def reduce_second(u):
        pair_copy(u).wait_recv()
        acc[u, core] = acc[u, core] + r1[u]
        for d in (2, 1, -1):
            ring_copy(u, d).start()

    def reduce_third(u):
        for d in (1, -1, 2):
            ring_copy(u, d).wait_recv()
        total = acc[u, core, y] + r2[u, 0] + r2[u, 1] + r2[u, 2]
        for b in range(4):
            pb[me * RING + b, pl.ds(u * 32, 32)] = total[:, b * BLK : (b + 1) * BLK]

    masked = False
    arrived = {(u, dp, dq): 0.0 for u in range(UNITS) for dp in (0, 1, -1, 2) for dq in (0, 1, -1, 2)}
    for u in range(UNITS):
        arrived[u, 0, 0] = 1.0
    ready = []
    left = {u: 4 for u in range(UNITS)}
    later = []
    for n, (c, started) in enumerate(GATHER):
        if c is not None:
            gather_copy(c).wait_recv()
            u, dp, dq = arrivals(c)
            arrived[u, dp, dq] += 1.0 if c[4] == 1 else 0.5
            if all(arrived[u, d, dq] == 1.0 for d in (0, 1, -1, 2)):
                ready.append((u, dq))
        for c in started:
            gather_copy(c).start()
        if not masked:
            load.wait()
            masked = True

            def tile(i, _):
                at = pl.ds(pl.multiple_of(i * BLK, BLK), BLK)
                for r in range(mask.shape[0]):
                    keep = mask[r, i].astype(jnp.float32).astype(jnp.bfloat16)
                    rows = pl.ds(r * BLK, BLK)
                    h_ref[rows, at] = h_ref[rows, at] * keep
                return 0

            lax.fori_loop(0, mask.shape[1], tile, 0)
        for due, do in [e for e in later if e[0] <= n]:
            do()
        later = [e for e in later if e[0] > n]
        for u, dq in ready:
            batch(u, dq)
            left[u] -= 1
            if left[u] == 0:
                pair_copy(u).start()
                later.append((n + 3, lambda u=u: reduce_second(u)))
                later.append((n + 7, lambda u=u: reduce_third(u)))
        ready = []

    def spread_step(h, n):
        c, started = SPREAD[n]
        if c is not None:
            spread_copy(h, c).wait_recv()
        for c in started:
            spread_copy(h, c).start()

    spread_step(0, 0)
    for n in range(1, 9):
        spread_step(0, n)
    later.sort(key=lambda e: e[0])
    for _, do in later[:2]:
        do()
    for n in range(9, 25):
        spread_step(0, n)
    for _, do in later[2:]:
        do()
    spread_step(1, 0)
    for n in range(25, len(SPREAD)):
        spread_step(0, n)
    for n in range(1, len(SPREAD)):
        spread_step(1, n)

    def one_pair(k, _):
        lt = pb[pairs[k, 0]]
        rt = pb[pairs[k, 1]]
        dots = lax.dot_general(
            lt, rt, (((0,), (0,)), ((), ())),
            precision=lax.Precision.HIGHEST, preferred_element_type=jnp.float32,
        )
        at = d_ref.at[(k // 2) % 2, k // 4, k % 2]
        at[0:BLK] = dots
        at[BLK : BLK + 8] = jnp.broadcast_to(jnp.sum(lt * lt, axis=0, keepdims=True), (8, BLK))
        at[BLK + 8 : BLK + 16] = jnp.broadcast_to(jnp.sum(rt * rt, axis=0, keepdims=True), (8, BLK))
        return 0

    lax.fori_loop(0, pairs.shape[0], one_pair, 0)
    swap = remote(d_ref.at[1 - core], e1, s3, v3, twin)
    swap.start()
    swap.wait_recv()

    def add(i, _):
        d_ref[core, i] = d_ref[core, i] + e1[i]
        return 0

    lax.fori_loop(0, RING, add, 0)

    def share_copy(d):
        i = {1: 0, -1: 1, 2: 2}[d]
        return remote(d_ref.at[core, wrap(y, d)], e2.at[i], us.at[i], uv.at[i], along_y(d))

    for d in (2, 1, -1):
        share_copy(d).start()
    for d in (1, -1, 2):
        share_copy(d).wait_recv()
    for j in range(2):
        total = d_ref[core, y, j] + e2[0, j] + e2[1, j] + e2[2, j]
        lscale = lax.rsqrt(total[BLK : BLK + 1] / P_SIZE + 1e-06)
        rscale = lax.rsqrt(total[BLK + 8 : BLK + 9] / P_SIZE + 1e-06)
        lfull = jnp.broadcast_to(lscale, (BLK, BLK)).T
        out[j] = total[0:BLK] / P_SIZE * lfull * rscale

    for c in GATHER_IDS:
        gather_copy(c).wait_send()
    for h in range(2):
        for c in SPREAD_IDS:
            spread_copy(h, c).wait_send()
    for u in range(UNITS):
        pair_copy(u).wait_send()
        for d in (1, -1, 2):
            ring_copy(u, d).wait_send()
    swap.wait_send()
    for d in (1, -1, 2):
        share_copy(d).wait_send()


def body(hist, tile_mask, planes, pairs):
    rows, depth = hist.shape
    cols = planes.shape[1] // UNITS
    f32 = jnp.float32
    dma = pltpu.SemaphoreType.DMA
    return pl.pallas_call(
        kernel,
        out_shape=jax.ShapeDtypeStruct((2, BLK, BLK), f32),
        in_specs=[
            pl.BlockSpec(memory_space=pl.ANY),
            pl.BlockSpec(memory_space=pl.ANY),
            pl.BlockSpec(memory_space=pltpu.SMEM),
            pl.BlockSpec(memory_space=pltpu.SMEM),
        ],
        out_specs=pl.BlockSpec(memory_space=pltpu.VMEM),
        scratch_shapes=[
            pltpu.VMEM((UNITS, RING * RING, cols, depth), jnp.bfloat16),
            pltpu.VMEM((rows, depth), jnp.bfloat16),
            pltpu.VMEM((UNITS, 2, RING, 2 * cols, rows), f32),
            pltpu.VMEM((UNITS, RING, 2 * cols, rows), f32),
            pltpu.VMEM((UNITS, 3, 2 * cols, rows), f32),
            pltpu.VMEM((RING * RING * RING, BLK, BLK), f32),
            pltpu.VMEM((2, RING, 2, BLK + 16, BLK), f32),
            pltpu.VMEM((RING, 2, BLK + 16, BLK), f32),
            pltpu.VMEM((3, 2, BLK + 16, BLK), f32),
            dma((UNITS,)),
            dma,
            dma((len(GATHER_IDS),)),
            dma((len(GATHER_IDS),)),
            dma((UNITS,)),
            dma((UNITS,)),
            dma((UNITS, 3)),
            dma((UNITS, 3)),
            dma,
            dma,
            dma((2, len(SPREAD_IDS))),
            dma((2, len(SPREAD_IDS))),
            dma((3,)),
            dma((3,)),
        ],
        compiler_params=pltpu.CompilerParams(
            collective_id=0, has_side_effects=True, vmem_limit_bytes=63 * 2**20
        ),
    )(planes.T, hist, tile_mask, pairs)


def solution(mesh):
    placed = (P("sess", "act"), P("sess", "act"), P("act", "sess"), P("sess", None))
    return jax.shard_map(
        body, mesh=mesh, in_specs=placed, out_specs=P(("sess", "act"), None, None), check_vma=False
    )
```

```python
import heapq

import jax
import jax.numpy as jnp
from jax import lax
from jax.experimental import pallas as pl
from jax.experimental.pallas import tpu as pltpu
from jax.sharding import PartitionSpec as P

MESH = pl.DeviceIdType.MESH
P_SIZE = 1024
RING = 4
UNITS = 4
BLK = 128
WAIT_PARTNER = 8
WAIT_HOME = 12


def simulate(todo, needs, rank, link, length, depth, latency=2.0, ready=()):
    todo = sorted(todo, key=rank)
    done, flying, free, count = set(), {}, {}, len(ready)
    events = [(at, i, mark) for i, (at, mark) in enumerate(ready)]
    heapq.heapify(events)

    def start(now):
        nonlocal count
        out = []
        for c in todo:
            if not all(d in done for d in needs(c)):
                continue
            way = link(c)
            flying[way] = [f for f in flying.get(way, []) if f > now]
            if len(flying[way]) >= depth:
                continue
            end = max(now, free.get(way, 0.0)) + length(c)
            free[way] = end
            flying[way].append(end)
            heapq.heappush(events, (end + latency, count, c))
            count += 1
            out.append(c)
        for c in out:
            todo.remove(c)
        return out

    order = [(None, start(0.0))]
    while events:
        now, _, c = heapq.heappop(events)
        done.add(c)
        order.append((c, start(now)))
    assert not todo
    simulate.end = now
    return order


MATE, PARTNER = 0, 1
MASKED = (-1, 0, 0, 0, 0)


def plan_gather():
    todo = [(k, 2, r, PARTNER, 1) for k in (0, 1) for r in range(4)]
    for u in range(2 * UNITS):
        todo += [(u, 0, 1, PARTNER, 1), (u, 0, 2, MATE, 1), (u, 0, 3, MATE, 1)]
        todo += [(u, 1, a, w, hop) for a in range(4) for w in (0, 1) for hop in (1, 2)]

    def needs(c):
        u, stage, a, w, hop = c
        if stage == 2:
            return [MASKED]
        if stage == 0:
            return [(u, 0, 1, PARTNER, 1)] if a == 3 else []
        if hop == 2:
            return [(u, 1, a, 1 - w, 1)]
        return [(u, 0, a, PARTNER if a == 1 else MATE, 1)] if a else []

    def rank(c):
        u, stage, a, w, hop = c
        if stage == 2:
            return (HIST_RANK[a], -1, a, 0, 0, u)
        return (u // 2, stage, a if stage == 0 else 0, 0 if stage == 0 else -a, hop, w, u)

    def link(c):
        u, stage, a, w, hop = c
        return (u + (stage == 1)) % 2

    def length(c):
        return 11.4 * (1.0 if c[1] == 2 else 0.125 / c[4])

    return simulate(todo, needs, rank, link, length, DEPTH, ready=[(9.0, MASKED)])


def plan_spread():
    todo = []
    for u in (0, 1):
        for s in (1, -1):
            for hop in (1, 2):
                todo.append((u, 0, 0, s, hop))
                todo += [(u, 1, dp, s, hop) for dp in (0, -1, 1, 2)]

    def needs(c):
        u, stage, dp, s, hop = c
        if hop == 2:
            return [(u, stage, dp, s, 1)]
        if stage == 0 or dp == 0:
            return []
        if dp == 2:
            return [(u, 0, 0, 1, 2), (u, 0, 0, -1, 2)]
        return [(u, 0, 0, -dp, 1)]

    def rank(c):
        u, stage, dp, s, hop = c
        far = {2: 2, -1: 1, 1: 1, 0: 0}[dp]
        return (stage, hop if stage == 0 else 0, far, hop, u, s)

    def link(c):
        return ((c[0] + c[1]) % 2, c[3])

    return simulate(todo, needs, rank, link, lambda c: 1.4 / c[4], 20)


HIST_RANK = (0, 0, 0, 0)
DEPTH = 10
GATHER = plan_gather()
SPREAD = plan_spread()
DIRECT = (UNITS - 1,)
PARTS = ((0, 96), (96, 32))


def numbered(order):
    ids = {}
    for _, started in order:
        for c in started:
            ids[c] = len(ids)
    return ids


GATHER_IDS = numbered(GATHER)
SPREAD_IDS = numbered(SPREAD)


def kernel(
    planes, hist, mask, pairs, out,
    g_ref, h_ref, hp, acc, accp, r1, r2, r3, r4, r5, pb, d_ref, e1, e2,
    own_sem, hist_sem, send, recv, s1, v1, s2, v2, s3, v3, s4, v4, s5, v5, s6, v6,
    ts, tv, us, uv,
):
    cols, depth = planes.shape[1:]
    half, quarter = depth // 2, depth // 4
    rows = h_ref.shape[0]
    me = lax.axis_index("sess")
    z, x = me // RING, me % RING
    act = lax.axis_index("act")
    y, core = act // 2, act % 2
    place = (z, x)

    def wrap(v, d):
        return lax.rem(v + d + RING, RING)

    def near(axis, d):
        return {"sess": wrap(z, d) * RING + x if axis == 0 else z * RING + wrap(x, d)}

    def along_y(d):
        return {"act": wrap(y, d) * 2 + core}

    twin = {"act": y * 2 + 1 - core}

    def remote(src, dst, send_sem, recv_sem, device):
        return pltpu.make_async_remote_copy(
            src_ref=src, dst_ref=dst, send_sem=send_sem, recv_sem=recv_sem,
            device_id=device, device_id_type=MESH,
        )

    def toward(axis, way):
        even = 1 - 2 * lax.rem(place[axis] + core, 2)
        return even if way == MATE else -even

    def beside(axis, way):
        return near(axis, toward(axis, way))

    group = [lax.rem(place[k] - core + RING, RING) // 2 for k in (0, 1)]
    keep_at = [pl.multiple_of(k * half + group[k] * quarter, quarter) for k in (0, 1)]
    give_at = [pl.multiple_of(k * half + (1 - group[k]) * quarter, quarter) for k in (0, 1)]

    around = [(a, d) for a in (0, 1) for d in (1, -1)]
    peers = [near(a, d) | {"act": y * 2 + c} for a, d in around for c in (0, 1)]
    peers += [along_y(d) for d in (1, -1, 2)] + [twin]
    barrier = pltpu.get_barrier_semaphore()
    for peer in peers:
        pl.semaphore_signal(barrier, inc=1, device_id=peer, device_id_type=MESH)

    pieces = give_at + keep_at
    loads = []
    for i, at in enumerate(pieces):
        at = pl.ds(at, quarter)
        loads.append(pltpu.make_async_copy(hist.at[:, at], h_ref.at[:, at], hist_sem.at[i]))
        loads[i].start()
    owns = []
    for k in (0, 1):
        src = planes.at[:, :, pl.ds(keep_at[k], quarter)]
        owns.append(pltpu.make_async_copy(src, g_ref.at[:, k, me], own_sem.at[k]))
        owns[k].start()
    pl.semaphore_wait(barrier, len(peers))

    def mask_piece(i):
        loads[i].wait()
        first = pieces[i] // BLK

        def tile(j, _):
            at = pl.ds(pl.multiple_of(pieces[i] + j * BLK, BLK), BLK)
            for r in range(mask.shape[0]):
                keep = mask[r, first + j].astype(jnp.float32).astype(jnp.bfloat16)
                some = pl.ds(r * BLK, BLK)
                h_ref[some, at] = h_ref[some, at] * keep
            return 0

        lax.fori_loop(0, quarter // BLK, tile, 0)

    def ends(c):
        u, stage, dp, s, hop = c
        pc, qc = place[u % 2], place[1 - u % 2]
        axis = (u + stage) % 2
        if stage == 0:
            return pc if hop == 1 else wrap(pc, -s), qc, near(axis, s)
        return wrap(pc, dp), qc if hop == 1 else wrap(qc, -s), near(axis, s)

    def slot(c, p, q):
        return p * RING + q if c[0] % 2 == 0 else q * RING + p

    def gather_copy(c):
        u, stage, a, w, hop = c
        i = GATHER_IDS[c]
        g, k = u // 2, u % 2
        if stage == 2:
            some = pl.ds(a * BLK, BLK)
            src = h_ref.at[some, pl.ds(give_at[k], quarter)]
            return remote(src, hp.at[k, some], send.at[i], recv.at[i], beside(k, w))
        pc, qc = place[k], place[1 - k]
        axis = k if stage == 0 else 1 - k
        if stage == 0:
            p, q = wrap(pc, toward(k, PARTNER)) if a == 3 else pc, qc
        else:
            steps = (0, toward(k, PARTNER), toward(k, MATE), 2)
            p, q = wrap(pc, steps[a]), qc
            if hop == 2:
                q = wrap(qc, toward(1 - k, 1 - w))
        ref = g_ref.at[g, k, slot(c, p, q)]
        src = ref
        if hop == 2:
            ref = src = ref.at[:, pl.ds(w * quarter // 2, quarter // 2)]
        elif stage == 0 and a == 1:
            src = planes.at[g, :, pl.ds(give_at[k], quarter)]
        elif a == 0 or (stage == 0 and a == 2):
            src = planes.at[g, :, pl.ds(keep_at[k], quarter)]
        return remote(src, ref, send.at[i], recv.at[i], beside(axis, w))

    def spread_copy(h, c):
        p, q, device = ends(c)
        at = slot(c, p, q) * RING + 2 * c[0]
        if c[4] == 2:
            rows = pl.ds(at if c[3] == 1 else at + 1, 1)
        else:
            rows = pl.ds(at, 2)
        ref = pb.at[rows, pl.ds(*PARTS[h])]
        i = SPREAD_IDS[c]
        return remote(ref, ref, ts.at[h, i], tv.at[h, i], device)

    shape = (RING, 2, 2 * cols, rows)

    def multiply(g, k, first):
        some = g_ref[g, k].reshape(RING * RING * cols, quarter)
        dims = (((1,), (1,)), ((), ()))
        mine = h_ref[:, pl.ds(keep_at[k], quarter)]
        total = lax.dot_general(some, mine, dims, preferred_element_type=jnp.float32)
        total = total.reshape(shape)
        acc[g] = total if first else acc[g] + total

    def multiply_partner(g, k):
        some = g_ref[g, k].reshape(RING * RING * cols, quarter)
        dims = (((1,), (1,)), ((), ()))
        total = lax.dot_general(some, hp[k], dims, preferred_element_type=jnp.float32)
        accp[g, k] = total.reshape(shape)

    turn = {1: 0, -1: 1, 2: 2}

    def pair_copy(g):
        return remote(acc.at[g, :, 1 - core], r1.at[g], s1.at[g], v1.at[g], twin)

    def ring_copy(g, d):
        i = turn[d]
        src = acc.at[g, wrap(y, d), core]
        return remote(src, r2.at[g, i], s2.at[g, i], v2.at[g, i], along_y(d))

    def partner_ring(g, k, d):
        i = turn[d]
        src = accp.at[g, k, wrap(y, d)]
        return remote(src, r3.at[g, k, i], s4.at[g, k, i], v4.at[g, k, i], along_y(d))

    def home_copy(g, k, c):
        target = beside(k, PARTNER) | {"act": y * 2 + c}
        return remote(
            accp.at[g, k, y, c], r4.at[g, core, k], s5.at[g, k, c], v5.at[g, core, k], target
        )

    def home_wait(g, k, c):
        sem = v5.at[g, c, k]
        remote(r4.at[g, c, k], r4.at[g, c, k], s5.at[g, k, c], sem, twin).wait_recv()

    def direct_copy(k):
        return remote(accp.at[UNITS - 1, k], r5.at[k], s6.at[k], v6.at[k], beside(k, PARTNER))

    def reduce_first(g):
        if g in DIRECT:
            for k in (0, 1):
                direct_copy(k).wait_recv()
            acc[g] = acc[g] + r5[0] + r5[1]
        pair_copy(g).start()

    def reduce_second(g):
        pair_copy(g).wait_recv()
        acc[g, :, core] = acc[g, :, core] + r1[g]
        for d in (2, 1, -1):
            ring_copy(g, d).start()

    def reduce_partner(g):
        if g in DIRECT:
            return
        for k in (0, 1):
            for d in (1, -1, 2):
                partner_ring(g, k, d).wait_recv()
            accp[g, k, y] = accp[g, k, y] + r3[g, k, 0] + r3[g, k, 1] + r3[g, k, 2]
            for c in (0, 1):
                home_copy(g, k, c).start()

    def reduce_third(g):
        for d in (1, -1, 2):
            ring_copy(g, d).wait_recv()
        total = acc[g, y, core] + r2[g, 0] + r2[g, 1] + r2[g, 2]
        if g not in DIRECT:
            for k in (0, 1):
                for c in (0, 1):
                    home_wait(g, k, c)
                    total = total + r4[g, c, k]
        for b in range(4):
            pb[me * RING + b, pl.ds(g * 32, 32)] = total[:, b * BLK : (b + 1) * BLK]

    def spread_steps(h, begin, end):
        for c, started in SPREAD[begin:end]:
            if c is not None:
                spread_copy(h, c).wait_recv()
            for c2 in started:
                spread_copy(h, c2).start()

    got = {u: 1.0 for u in range(2 * UNITS)}
    tiles = {0: 0, 1: 0}
    waiting, seen, later = [], set(), []
    steps = len(SPREAD)
    last = max(n for n, (_, started) in enumerate(GATHER) if started)
    for n, (c, started) in enumerate(GATHER):
        if c == MASKED:
            mask_piece(0)
            mask_piece(1)
        elif c is not None:
            gather_copy(c).wait_recv()
            if c[1] == 2:
                tiles[c[0]] += 1
            else:
                got[c[0]] += 1.0 / c[4]
                if got[c[0]] == 16.0:
                    waiting.append(c[0])
        for c2 in started:
            gather_copy(c2).start()
        if c == MASKED:
            mask_piece(2)
            mask_piece(3)
            owns[0].wait()
            owns[1].wait()
        for due, do in [e for e in later if e[0] <= n]:
            do()
        later = [e for e in later if e[0] > n]
        if n == last:
            assert not later, later
            spread_steps(0, 0, 1)
        for u in [u for u in waiting if tiles[u % 2] == 4]:
            waiting.remove(u)
            g, k = u // 2, u % 2
            multiply_partner(g, k)
            if g in DIRECT:
                direct_copy(k).start()
            else:
                for d in (2, 1, -1):
                    partner_ring(g, k, d).start()
            multiply(g, k, g not in seen)
            if g in seen:
                if g in DIRECT:
                    assert n >= len(GATHER) - 4
                    later.append((n, lambda g=g: reduce_first(g)))
                else:
                    reduce_first(g)
                later.append((n + 4, lambda g=g: reduce_second(g)))
                later.append((n + WAIT_PARTNER, lambda g=g: reduce_partner(g)))
                later.append((n + WAIT_HOME, lambda g=g: reduce_third(g)))
            seen.add(g)

    later.sort(key=lambda e: e[0])
    assert not waiting and len(later) == 4
    later.pop(0)[1]()
    spread_steps(0, 1, 9)
    later[0][1]()
    spread_steps(0, 9, 25)
    later[2][1]()
    spread_steps(1, 0, 1)
    spread_steps(0, 25, steps)
    spread_steps(1, 1, steps)

    def one_pair(k, _):
        lt = pb[pairs[k, 0]]
        rt = pb[pairs[k, 1]]
        dots = lax.dot_general(
            lt, rt, (((0,), (0,)), ((), ())),
            precision=lax.Precision.HIGHEST, preferred_element_type=jnp.float32,
        )
        at = d_ref.at[(k // 2) % 2, k // 4, k % 2]
        at[0:BLK] = dots
        at[BLK : BLK + 8] = jnp.broadcast_to(jnp.sum(lt * lt, axis=0, keepdims=True), (8, BLK))
        at[BLK + 8 : BLK + 16] = jnp.broadcast_to(jnp.sum(rt * rt, axis=0, keepdims=True), (8, BLK))
        return 0

    lax.fori_loop(0, pairs.shape[0], one_pair, 0, unroll=4)
    swap = remote(d_ref.at[1 - core], e1, s3, v3, twin)
    swap.start()
    swap.wait_recv()

    def add(i, _):
        d_ref[core, i] = d_ref[core, i] + e1[i]
        return 0

    lax.fori_loop(0, RING, add, 0)

    def share_copy(d):
        i = {1: 0, -1: 1, 2: 2}[d]
        return remote(d_ref.at[core, wrap(y, d)], e2.at[i], us.at[i], uv.at[i], along_y(d))

    for d in (2, 1, -1):
        share_copy(d).start()
    for d in (1, -1, 2):
        share_copy(d).wait_recv()
    for j in range(2):
        total = d_ref[core, y, j] + e2[0, j] + e2[1, j] + e2[2, j]
        lscale = lax.rsqrt(total[BLK : BLK + 1] / P_SIZE + 1e-06)
        rscale = lax.rsqrt(total[BLK + 8 : BLK + 9] / P_SIZE + 1e-06)
        lfull = jnp.broadcast_to(lscale, (BLK, BLK)).T
        out[j] = total[0:BLK] / P_SIZE * lfull * rscale

    for c in GATHER_IDS:
        gather_copy(c).wait_send()
    for h in range(2):
        for c in SPREAD_IDS:
            spread_copy(h, c).wait_send()
    for g in range(UNITS):
        pair_copy(g).wait_send()
        for d in (1, -1, 2):
            ring_copy(g, d).wait_send()
        for k in (0, 1):
            if g in DIRECT:
                direct_copy(k).wait_send()
                continue
            for d in (1, -1, 2):
                partner_ring(g, k, d).wait_send()
            for c in (0, 1):
                home_copy(g, k, c).wait_send()
    swap.wait_send()
    for d in (1, -1, 2):
        share_copy(d).wait_send()


def body(hist, tile_mask, planes, pairs):
    rows, depth = hist.shape
    cols = planes.shape[1] // UNITS
    f32 = jnp.float32
    dma = pltpu.SemaphoreType.DMA
    return pl.pallas_call(
        kernel,
        out_shape=jax.ShapeDtypeStruct((2, BLK, BLK), f32),
        in_specs=[
            pl.BlockSpec(memory_space=pl.ANY),
            pl.BlockSpec(memory_space=pl.ANY),
            pl.BlockSpec(memory_space=pltpu.SMEM),
            pl.BlockSpec(memory_space=pltpu.SMEM),
        ],
        out_specs=pl.BlockSpec(memory_space=pltpu.VMEM),
        scratch_shapes=[
            pltpu.VMEM((UNITS, 2, RING * RING, cols, depth // 4), jnp.bfloat16),
            pltpu.VMEM((rows, depth), jnp.bfloat16),
            pltpu.VMEM((2, rows, depth // 4), jnp.bfloat16),
            pltpu.VMEM((UNITS, RING, 2, 2 * cols, rows), f32),
            pltpu.VMEM((UNITS, 2, RING, 2, 2 * cols, rows), f32),
            pltpu.VMEM((UNITS, RING, 2 * cols, rows), f32),
            pltpu.VMEM((UNITS, 3, 2 * cols, rows), f32),
            pltpu.VMEM((UNITS - 1, 2, 3, 2, 2 * cols, rows), f32),
            pltpu.VMEM((UNITS - 1, 2, 2, 2 * cols, rows), f32),
            pltpu.VMEM((2, RING, 2, 2 * cols, rows), f32),
            pltpu.VMEM((RING * RING * RING, BLK, BLK), f32),
            pltpu.VMEM((2, RING, 2, BLK + 16, BLK), f32),
            pltpu.VMEM((RING, 2, BLK + 16, BLK), f32),
            pltpu.VMEM((3, 2, BLK + 16, BLK), f32),
            dma((2,)),
            dma((4,)),
            dma((len(GATHER_IDS),)),
            dma((len(GATHER_IDS),)),
            dma((UNITS,)),
            dma((UNITS,)),
            dma((UNITS, 3)),
            dma((UNITS, 3)),
            dma,
            dma,
            dma((UNITS - 1, 2, 3)),
            dma((UNITS - 1, 2, 3)),
            dma((UNITS - 1, 2, 2)),
            dma((UNITS - 1, 2, 2)),
            dma((2,)),
            dma((2,)),
            dma((2, len(SPREAD_IDS))),
            dma((2, len(SPREAD_IDS))),
            dma((3,)),
            dma((3,)),
        ],
        compiler_params=pltpu.CompilerParams(
            collective_id=0, has_side_effects=True, vmem_limit_bytes=63 * 2**20
        ),
    )(planes.T.reshape(UNITS, cols, depth), hist, tile_mask, pairs)


def solution(mesh):
    placed = (P("sess", "act"), P("sess", "act"), P("act", "sess"), P("sess", None))
    return jax.shard_map(
        body, mesh=mesh, in_specs=placed, out_specs=P(("sess", "act"), None, None), check_vma=False
    )
```

```python
import heapq

import jax
import jax.numpy as jnp
from jax import lax
from jax.experimental import pallas as pl
from jax.experimental.pallas import tpu as pltpu
from jax.sharding import PartitionSpec as P

MESH = pl.DeviceIdType.MESH
P_SIZE = 1024
RING = 4
UNITS = 4
BLK = 128
WAIT_PARTNER = 24
WAIT_HOME = 32


def simulate(todo, needs, rank, link, length, depth, latency=2.0, ready=()):
    todo = sorted(todo, key=rank)
    done, flying, free, count = set(), {}, {}, len(ready)
    events = [(at, i, mark) for i, (at, mark) in enumerate(ready)]
    heapq.heapify(events)

    def start(now):
        nonlocal count
        out = []
        for c in todo:
            if not all(d in done for d in needs(c)):
                continue
            way = link(c)
            flying[way] = [f for f in flying.get(way, []) if f > now]
            if len(flying[way]) >= depth:
                continue
            end = max(now, free.get(way, 0.0)) + length(c)
            free[way] = end
            flying[way].append(end)
            heapq.heappush(events, (end + latency, count, c))
            count += 1
            out.append(c)
        for c in out:
            todo.remove(c)
        return out

    order = [(None, start(0.0))]
    while events:
        now, _, c = heapq.heappop(events)
        done.add(c)
        order.append((c, start(now)))
    assert not todo
    simulate.end = now
    return order


MATE, PARTNER = 0, 1
MASKED = (-1, 0, 0, 0, 0)


def plan_gather():
    todo = [(k, 2, r, PARTNER, 1) for k in (0, 1) for r in range(4)]
    for u in range(2 * UNITS):
        todo += [(u, 0, 1, PARTNER, 1), (u, 0, 2, MATE, 1), (u, 0, 3, MATE, 1)]
        todo += [(u, 1, a, w, hop) for a in range(4) for w in (0, 1) for hop in (1, 2)]

    def needs(c):
        u, stage, a, w, hop = c
        if stage == 2:
            return [MASKED]
        if stage == 0:
            return [(u, 0, 1, PARTNER, 1)] if a == 3 else []
        if hop == 2:
            return [(u, 1, a, 1 - w, 1)]
        return [(u, 0, a, PARTNER if a == 1 else MATE, 1)] if a else []

    def rank(c):
        u, stage, a, w, hop = c
        if stage == 2:
            return (HIST_RANK[a], -1, a, 0, 0, u)
        return (u // 2, stage, a if stage == 0 else 0, 0 if stage == 0 else -a, hop, w, u)

    def link(c):
        u, stage, a, w, hop = c
        return (u + (stage == 1)) % 2

    def length(c):
        return 11.4 * (1.0 if c[1] == 2 else 0.125 / c[4])

    return simulate(todo, needs, rank, link, length, DEPTH, ready=[(9.0, MASKED)])


def plan_spread():
    todo = []
    for u in (0, 1):
        for s in (1, -1):
            for hop in (1, 2):
                todo.append((u, 0, 0, s, hop))
                todo += [(u, 1, dp, s, hop) for dp in (0, -1, 1, 2)]

    def needs(c):
        u, stage, dp, s, hop = c
        if hop == 2:
            return [(u, stage, dp, s, 1)]
        if stage == 0 or dp == 0:
            return []
        if dp == 2:
            return [(u, 0, 0, 1, 2), (u, 0, 0, -1, 2)]
        return [(u, 0, 0, -dp, 1)]

    def rank(c):
        u, stage, dp, s, hop = c
        far = {2: 2, -1: 1, 1: 1, 0: 0}[dp]
        return (stage, hop if stage == 0 else 0, far, hop, u, s)

    def link(c):
        return ((c[0] + c[1]) % 2, c[3])

    return simulate(todo, needs, rank, link, lambda c: 1.4 / c[4], 20)


HIST_RANK = (0, 0, 0, 0)
DEPTH = 10
TAIL = (4, 7, 9, 15, 27)
GATHER = plan_gather()
SPREAD = plan_spread()
RINGED = 2
PARTS = ((0, 112), (112, 48))
LEVELS = 512.0
TOP = 32767.0


def encode(values):
    most = jnp.maximum(jnp.max(jnp.abs(values), axis=0, keepdims=True), 1e-18)
    level = jnp.floor(jnp.log2(most) * LEVELS) + 2.0
    codes = jnp.round(values * (TOP * jnp.exp2(level * (-1.0 / LEVELS))))
    return codes.astype(jnp.int32).astype(jnp.int16), level


def level_rows(levels):
    row = lax.broadcasted_iota(jnp.int32, (16, levels[0].shape[1]), 0)
    tile = jnp.broadcast_to(levels[-1], row.shape)
    for i, level in enumerate(levels[:-1]):
        tile = jnp.where(row == i, level, tile)
    return tile.astype(jnp.int32).astype(jnp.int16)


def decode(codes, level):
    step = jnp.exp2(level * (1.0 / LEVELS)) * (1.0 / TOP)
    return codes.astype(jnp.int32).astype(jnp.float32) * step


def numbered(order):
    ids = {}
    for _, started in order:
        for c in started:
            ids[c] = len(ids)
    return ids


GATHER_IDS = numbered(GATHER)
SPREAD_IDS = numbered(SPREAD)


def kernel(
    planes, hist, mask, pairs, out,
    g_ref, h_ref, hp, acc, accp, r1, r2, r3, r4, dq, r5, pb, d_ref, e1, e2,
    own_sem, hist_sem, send, recv, s1, v1, s2, v2, s3, v3, s4, v4, s5, v5, s6, v6,
    ts, tv, us, uv,
):
    cols, depth = planes.shape[1:]
    half, quarter = depth // 2, depth // 4
    rows = h_ref.shape[0]
    me = lax.axis_index("sess")
    z, x = me // RING, me % RING
    act = lax.axis_index("act")
    y, core = act // 2, act % 2
    place = (z, x)

    def wrap(v, d):
        return lax.rem(v + d + RING, RING)

    def near(axis, d):
        return {"sess": wrap(z, d) * RING + x if axis == 0 else z * RING + wrap(x, d)}

    def along_y(d):
        return {"act": wrap(y, d) * 2 + core}

    twin = {"act": y * 2 + 1 - core}

    def remote(src, dst, send_sem, recv_sem, device):
        return pltpu.make_async_remote_copy(
            src_ref=src, dst_ref=dst, send_sem=send_sem, recv_sem=recv_sem,
            device_id=device, device_id_type=MESH,
        )

    def toward(axis, way):
        even = 1 - 2 * lax.rem(place[axis] + core, 2)
        return even if way == MATE else -even

    def beside(axis, way):
        return near(axis, toward(axis, way))

    group = [lax.rem(place[k] - core + RING, RING) // 2 for k in (0, 1)]
    keep_at = [pl.multiple_of(k * half + group[k] * quarter, quarter) for k in (0, 1)]
    give_at = [pl.multiple_of(k * half + (1 - group[k]) * quarter, quarter) for k in (0, 1)]

    around = [(a, d) for a in (0, 1) for d in (1, -1)]
    peers = [near(a, d) | {"act": y * 2 + c} for a, d in around for c in (0, 1)]
    peers += [along_y(d) for d in (1, -1, 2)] + [twin]
    barrier = pltpu.get_barrier_semaphore()
    for peer in peers:
        pl.semaphore_signal(barrier, inc=1, device_id=peer, device_id_type=MESH)

    pieces = give_at + keep_at
    loads = []
    for i, at in enumerate(pieces):
        at = pl.ds(at, quarter)
        loads.append(pltpu.make_async_copy(hist.at[:, at], h_ref.at[:, at], hist_sem.at[i]))
        loads[i].start()
    owns = []
    for k in (0, 1):
        src = planes.at[:, :, pl.ds(keep_at[k], quarter)]
        owns.append(pltpu.make_async_copy(src, g_ref.at[:, k, me], own_sem.at[k]))
        owns[k].start()
    pl.semaphore_wait(barrier, len(peers))

    def mask_piece(i):
        loads[i].wait()
        first = pieces[i] // BLK

        def tile(j, _):
            at = pl.ds(pl.multiple_of(pieces[i] + j * BLK, BLK), BLK)
            for r in range(mask.shape[0]):
                keep = mask[r, first + j].astype(jnp.float32).astype(jnp.bfloat16)
                some = pl.ds(r * BLK, BLK)
                h_ref[some, at] = h_ref[some, at] * keep
            return 0

        lax.fori_loop(0, quarter // BLK, tile, 0)

    def ends(c):
        u, stage, dp, s, hop = c
        pc, qc = place[u % 2], place[1 - u % 2]
        axis = (u + stage) % 2
        if stage == 0:
            return pc if hop == 1 else wrap(pc, -s), qc, near(axis, s)
        return wrap(pc, dp), qc if hop == 1 else wrap(qc, -s), near(axis, s)

    def slot(c, p, q):
        return p * RING + q if c[0] % 2 == 0 else q * RING + p

    def gather_copy(c):
        u, stage, a, w, hop = c
        i = GATHER_IDS[c]
        g, k = u // 2, u % 2
        if stage == 2:
            some = pl.ds(a * BLK, BLK)
            src = h_ref.at[some, pl.ds(give_at[k], quarter)]
            return remote(src, hp.at[k, some], send.at[i], recv.at[i], beside(k, w))
        pc, qc = place[k], place[1 - k]
        axis = k if stage == 0 else 1 - k
        if stage == 0:
            p, q = wrap(pc, toward(k, PARTNER)) if a == 3 else pc, qc
        else:
            steps = (0, toward(k, PARTNER), toward(k, MATE), 2)
            p, q = wrap(pc, steps[a]), qc
            if hop == 2:
                q = wrap(qc, toward(1 - k, 1 - w))
        ref = g_ref.at[g, k, slot(c, p, q)]
        src = ref
        if hop == 2:
            ref = src = ref.at[:, pl.ds(w * quarter // 2, quarter // 2)]
        elif stage == 0 and a == 1:
            src = planes.at[g, :, pl.ds(give_at[k], quarter)]
        elif a == 0 or (stage == 0 and a == 2):
            src = planes.at[g, :, pl.ds(keep_at[k], quarter)]
        return remote(src, ref, send.at[i], recv.at[i], beside(axis, w))

    def spread_copy(h, c):
        p, q, device = ends(c)
        at = slot(c, p, q) * RING + 2 * c[0]
        if c[4] == 2:
            rows = pl.ds(at if c[3] == 1 else at + 1, 1)
        else:
            rows = pl.ds(at, 2)
        ref = pb.at[rows, pl.ds(*PARTS[h])]
        i = SPREAD_IDS[c]
        return remote(ref, ref, ts.at[h, i], tv.at[h, i], device)

    shape = (RING, 2, 2 * cols, rows)

    def multiply(g, k, first):
        some = g_ref[g, k].reshape(RING * RING * cols, quarter)
        dims = (((1,), (1,)), ((), ()))
        mine = h_ref[:, pl.ds(keep_at[k], quarter)]
        total = lax.dot_general(some, mine, dims, preferred_element_type=jnp.float32)
        total = total.reshape(shape)
        acc[g] = total if first else acc[g] + total

    def multiply_partner(g, k):
        some = g_ref[g, k].reshape(RING * RING * cols, quarter)
        dims = (((1,), (1,)), ((), ()))
        total = lax.dot_general(some, hp[k], dims, preferred_element_type=jnp.float32)
        if g < RINGED:
            accp[g, k] = total.reshape(shape)
        else:
            codes, level = encode(total)
            dq[g - RINGED, k, 0 : codes.shape[0]] = codes
            dq[g - RINGED, k, codes.shape[0] :] = level_rows([level])

    turn = {1: 0, -1: 1, 2: 2}

    def pair_copy(g):
        return remote(acc.at[g, :, 1 - core], r1.at[g], s1.at[g], v1.at[g], twin)

    def ring_copy(g, d):
        i = turn[d]
        src = acc.at[g, wrap(y, d), core]
        return remote(src, r2.at[g, i], s2.at[g, i], v2.at[g, i], along_y(d))

    def partner_ring(g, k, d):
        i = turn[d]
        src = accp.at[g, k, wrap(y, d)]
        return remote(src, r3.at[g, k, i], s4.at[g, k, i], v4.at[g, k, i], along_y(d))

    def home_copy(g, k, c):
        target = beside(k, PARTNER) | {"act": y * 2 + c}
        return remote(
            accp.at[g, k, y, c], r4.at[g, core, k], s5.at[g, k, c], v5.at[g, core, k], target
        )

    def home_wait(g, k, c):
        sem = v5.at[g, c, k]
        remote(r4.at[g, c, k], r4.at[g, c, k], s5.at[g, k, c], sem, twin).wait_recv()

    def direct_copy(g, k):
        i = g - RINGED
        return remote(dq.at[i, k], r5.at[i, k], s6.at[i, k], v6.at[i, k], beside(k, PARTNER))

    def reduce_first(g):
        if g >= RINGED:
            for k in (0, 1):
                direct_copy(g, k).wait_recv()
                many = RING * RING * cols
                level = r5[g - RINGED, k, many:].astype(jnp.int32).astype(jnp.float32)[0:1]
                acc[g] = acc[g] + decode(r5[g - RINGED, k, 0:many], level).reshape(shape)
        pair_copy(g).start()

    def reduce_second(g):
        pair_copy(g).wait_recv()
        acc[g, :, core] = acc[g, :, core] + r1[g]
        for d in (2, 1, -1):
            ring_copy(g, d).start()

    def reduce_partner(g):
        if g >= RINGED:
            return
        for k in (0, 1):
            for d in (1, -1, 2):
                partner_ring(g, k, d).wait_recv()
            accp[g, k, y] = accp[g, k, y] + r3[g, k, 0] + r3[g, k, 1] + r3[g, k, 2]
            for c in (0, 1):
                home_copy(g, k, c).start()

    def reduce_third(g):
        for d in (1, -1, 2):
            ring_copy(g, d).wait_recv()
        total = acc[g, y, core] + r2[g, 0] + r2[g, 1] + r2[g, 2]
        if g < RINGED:
            for k in (0, 1):
                for c in (0, 1):
                    home_wait(g, k, c)
                    total = total + r4[g, c, k]
        codes, level = encode(total)
        levels.append(level)
        last_of = g >= UNITS - 2
        at = g * 32 if g < UNITS - 1 else PARTS[1][0]
        tile = level_rows(levels[-1:] if g == UNITS - 1 else levels) if last_of else None
        for b in range(4):
            some = slice(b * BLK, (b + 1) * BLK)
            pb[me * RING + b, at : at + 32] = codes[:, some]
            if last_of:
                end = at + 32
                pb[me * RING + b, end : end + 16] = tile[:, some]

    levels = []

    def spread_steps(h, begin, end):
        for c, started in SPREAD[begin:end]:
            if c is not None:
                spread_copy(h, c).wait_recv()
            for c2 in started:
                spread_copy(h, c2).start()

    got = {u: 1.0 for u in range(2 * UNITS)}
    tiles = {0: 0, 1: 0}
    waiting, seen, later, held = [], set(), [], []
    steps = len(SPREAD)
    last = max(n for n, (_, started) in enumerate(GATHER) if started)
    for n, (c, started) in enumerate(GATHER):
        if c == MASKED:
            mask_piece(0)
            mask_piece(1)
        elif c is not None:
            gather_copy(c).wait_recv()
            if c[1] == 2:
                tiles[c[0]] += 1
            else:
                got[c[0]] += 1.0 / c[4]
                if got[c[0]] == 16.0:
                    waiting.append(c[0])
        for c2 in started:
            gather_copy(c2).start()
        if c == MASKED:
            mask_piece(2)
            mask_piece(3)
            owns[0].wait()
            owns[1].wait()
        for due, do in [e for e in later if e[0] <= n]:
            do()
        later = [e for e in later if e[0] > n]
        if n == last:
            assert not later, later
            spread_steps(0, 0, 1)
        for u in [u for u in waiting if tiles[u % 2] == 4]:
            waiting.remove(u)
            g, k = u // 2, u % 2
            multiply_partner(g, k)
            if g >= RINGED:
                direct_copy(g, k).start()
            else:
                for d in (2, 1, -1):
                    partner_ring(g, k, d).start()
            if g == UNITS - 1:
                held.append(k)
                continue
            multiply(g, k, g not in seen)
            if g in seen and g >= RINGED:
                later.append((n + 6, lambda g=g: reduce_first(g)))
                later.append((n + 10, lambda g=g: reduce_second(g)))
                later.append((n + 17, lambda g=g: reduce_third(g)))
            elif g in seen:
                reduce_first(g)
                later.append((n + 4, lambda g=g: reduce_second(g)))
                later.append((n + WAIT_PARTNER, lambda g=g: reduce_partner(g)))
                later.append((n + WAIT_HOME, lambda g=g: reduce_third(g)))
            seen.add(g)

    assert not waiting and not later and len(held) == 2
    g = UNITS - 1
    spread_steps(0, 1, TAIL[0])
    multiply(g, held[0], True)
    spread_steps(0, TAIL[0], TAIL[1])
    multiply(g, held[1], False)
    spread_steps(0, TAIL[1], TAIL[2])
    reduce_first(g)
    spread_steps(0, TAIL[2], TAIL[3])
    reduce_second(g)
    spread_steps(0, TAIL[3], TAIL[4])
    reduce_third(g)
    spread_steps(1, 0, 1)
    spread_steps(0, TAIL[4], steps)
    spread_steps(1, 1, steps)

    def one_pair(k, _):
        def block(i):
            level = pb[i, 96:112].astype(jnp.int32).astype(jnp.float32)
            out = [decode(pb[i, g * 32 : (g + 1) * 32], level[g : g + 1]) for g in range(3)]
            level = pb[i, 144:160].astype(jnp.int32).astype(jnp.float32)
            out.append(decode(pb[i, 112:144], level[0:1]))
            return jnp.concatenate(out, axis=0)

        lt = block(pairs[k, 0])
        rt = block(pairs[k, 1])
        dots = lax.dot_general(
            lt, rt, (((0,), (0,)), ((), ())),
            precision=lax.Precision.HIGHEST, preferred_element_type=jnp.float32,
        )
        at = d_ref.at[(k // 2) % 2, k // 4, k % 2]
        at[0:BLK] = dots
        at[BLK : BLK + 8] = jnp.broadcast_to(jnp.sum(lt * lt, axis=0, keepdims=True), (8, BLK))
        at[BLK + 8 : BLK + 16] = jnp.broadcast_to(jnp.sum(rt * rt, axis=0, keepdims=True), (8, BLK))
        return 0

    lax.fori_loop(0, pairs.shape[0], one_pair, 0, unroll=4)
    swap = remote(d_ref.at[1 - core], e1, s3, v3, twin)
    swap.start()
    swap.wait_recv()

    def add(i, _):
        d_ref[core, i] = d_ref[core, i] + e1[i]
        return 0

    lax.fori_loop(0, RING, add, 0)

    def share_copy(d):
        i = {1: 0, -1: 1, 2: 2}[d]
        return remote(d_ref.at[core, wrap(y, d)], e2.at[i], us.at[i], uv.at[i], along_y(d))

    for d in (2, 1, -1):
        share_copy(d).start()
    for d in (1, -1, 2):
        share_copy(d).wait_recv()
    for j in range(2):
        total = d_ref[core, y, j] + e2[0, j] + e2[1, j] + e2[2, j]
        lscale = lax.rsqrt(total[BLK : BLK + 1] / P_SIZE + 1e-06)
        rscale = lax.rsqrt(total[BLK + 8 : BLK + 9] / P_SIZE + 1e-06)
        lfull = jnp.broadcast_to(lscale, (BLK, BLK)).T
        out[j] = total[0:BLK] / P_SIZE * lfull * rscale

    for c in GATHER_IDS:
        gather_copy(c).wait_send()
    for h in range(2):
        for c in SPREAD_IDS:
            spread_copy(h, c).wait_send()
    for g in range(UNITS):
        pair_copy(g).wait_send()
        for d in (1, -1, 2):
            ring_copy(g, d).wait_send()
        for k in (0, 1):
            if g >= RINGED:
                direct_copy(g, k).wait_send()
                continue
            for d in (1, -1, 2):
                partner_ring(g, k, d).wait_send()
            for c in (0, 1):
                home_copy(g, k, c).wait_send()
    swap.wait_send()
    for d in (1, -1, 2):
        share_copy(d).wait_send()


def body(hist, tile_mask, planes, pairs):
    rows, depth = hist.shape
    cols = planes.shape[1] // UNITS
    f32 = jnp.float32
    dma = pltpu.SemaphoreType.DMA
    return pl.pallas_call(
        kernel,
        out_shape=jax.ShapeDtypeStruct((2, BLK, BLK), f32),
        in_specs=[
            pl.BlockSpec(memory_space=pl.ANY),
            pl.BlockSpec(memory_space=pl.ANY),
            pl.BlockSpec(memory_space=pltpu.SMEM),
            pl.BlockSpec(memory_space=pltpu.SMEM),
        ],
        out_specs=pl.BlockSpec(memory_space=pltpu.VMEM),
        scratch_shapes=[
            pltpu.VMEM((UNITS, 2, RING * RING, cols, depth // 4), jnp.bfloat16),
            pltpu.VMEM((rows, depth), jnp.bfloat16),
            pltpu.VMEM((2, rows, depth // 4), jnp.bfloat16),
            pltpu.VMEM((UNITS, RING, 2, 2 * cols, rows), f32),
            pltpu.VMEM((RINGED, 2, RING, 2, 2 * cols, rows), f32),
            pltpu.VMEM((UNITS, RING, 2 * cols, rows), f32),
            pltpu.VMEM((UNITS, 3, 2 * cols, rows), f32),
            pltpu.VMEM((RINGED, 2, 3, 2, 2 * cols, rows), f32),
            pltpu.VMEM((RINGED, 2, 2, 2 * cols, rows), f32),
            pltpu.VMEM((UNITS - RINGED, 2, RING * RING * cols + 16, rows), jnp.int16),
            pltpu.VMEM((UNITS - RINGED, 2, RING * RING * cols + 16, rows), jnp.int16),
            pltpu.VMEM((RING * RING * RING, 160, BLK), jnp.int16),
            pltpu.VMEM((2, RING, 2, BLK + 16, BLK), f32),
            pltpu.VMEM((RING, 2, BLK + 16, BLK), f32),
            pltpu.VMEM((3, 2, BLK + 16, BLK), f32),
            dma((2,)),
            dma((4,)),
            dma((len(GATHER_IDS),)),
            dma((len(GATHER_IDS),)),
            dma((UNITS,)),
            dma((UNITS,)),
            dma((UNITS, 3)),
            dma((UNITS, 3)),
            dma,
            dma,
            dma((RINGED, 2, 3)),
            dma((RINGED, 2, 3)),
            dma((RINGED, 2, 2)),
            dma((RINGED, 2, 2)),
            dma((UNITS - RINGED, 2)),
            dma((UNITS - RINGED, 2)),
            dma((2, len(SPREAD_IDS))),
            dma((2, len(SPREAD_IDS))),
            dma((3,)),
            dma((3,)),
        ],
        compiler_params=pltpu.CompilerParams(
            collective_id=0, has_side_effects=True, vmem_limit_bytes=63 * 2**20
        ),
    )(planes.T.reshape(UNITS, cols, depth), hist, tile_mask, pairs)


def solution(mesh):
    placed = (P("sess", "act"), P("sess", "act"), P("act", "sess"), P("sess", None))
    return jax.shard_map(
        body, mesh=mesh, in_specs=placed, out_specs=P(("sess", "act"), None, None), check_vma=False
    )
```

```python
import heapq

import jax
import jax.numpy as jnp
from jax import lax
from jax.experimental import pallas as pl
from jax.experimental.pallas import tpu as pltpu
from jax.sharding import PartitionSpec as P

MESH = pl.DeviceIdType.MESH
P_SIZE = 1024
RING = 4
UNITS = 4
BLK = 128
WAIT_PARTNER = 32
WAIT_HOME = 42


def simulate(todo, needs, rank, link, length, depth, latency=2.0, ready=()):
    todo = sorted(todo, key=rank)
    done, flying, free, count = set(), {}, {}, len(ready)
    events = [(at, i, mark) for i, (at, mark) in enumerate(ready)]
    heapq.heapify(events)

    def start(now):
        nonlocal count
        out = []
        for c in todo:
            if not all(d in done for d in needs(c)):
                continue
            way = link(c)
            flying[way] = [f for f in flying.get(way, []) if f > now]
            if len(flying[way]) >= depth:
                continue
            end = max(now, free.get(way, 0.0)) + length(c)
            free[way] = end
            flying[way].append(end)
            heapq.heappush(events, (end + latency, count, c))
            count += 1
            out.append(c)
        for c in out:
            todo.remove(c)
        return out

    order = [(None, start(0.0))]
    while events:
        now, _, c = heapq.heappop(events)
        done.add(c)
        order.append((c, start(now)))
    assert not todo
    simulate.end = now
    return order


MATE, PARTNER = 0, 1
MASKED = (-1, 0, 0, 0, 0)


def plan_gather():
    todo = [(k, 2, r, PARTNER, 1) for k in (0, 1) for r in range(4)]
    for u in range(2 * UNITS):
        todo += [(u, 0, 1, PARTNER, 1), (u, 0, 2, MATE, 1), (u, 0, 3, MATE, 1)]
        todo += [(u, 1, a, w, hop) for a in range(4) for w in (0, 1) for hop in (1, 2)]

    def needs(c):
        u, stage, a, w, hop = c
        if stage == 2:
            return [MASKED]
        if stage == 0:
            return [(u, 0, 1, PARTNER, 1)] if a == 3 else []
        if hop == 2:
            return [(u, 1, a, 1 - w, 1)]
        return [(u, 0, a, PARTNER if a == 1 else MATE, 1)] if a else []

    def rank(c):
        u, stage, a, w, hop = c
        if stage == 2:
            return (HIST_RANK[a], -1, a, 0, 0, u)
        return (u // 2, stage, a if stage == 0 else 0, 0 if stage == 0 else -a, hop, w, u)

    def link(c):
        u, stage, a, w, hop = c
        return (u + (stage == 1)) % 2

    def length(c):
        return 11.4 * (1.0 if c[1] == 2 else 0.125 / c[4])

    return simulate(todo, needs, rank, link, length, DEPTH, ready=[(9.0, MASKED)])


def plan_spread():
    todo = []
    for u in (0, 1):
        for s in (1, -1):
            for hop in (1, 2):
                todo.append((u, 0, 0, s, hop))
                todo += [(u, 1, dp, s, hop) for dp in (0, -1, 1, 2)]

    def needs(c):
        u, stage, dp, s, hop = c
        if hop == 2:
            return [(u, stage, dp, s, 1)]
        if stage == 0 or dp == 0:
            return []
        if dp == 2:
            return [(u, 0, 0, 1, 2), (u, 0, 0, -1, 2)]
        return [(u, 0, 0, -dp, 1)]

    def rank(c):
        u, stage, dp, s, hop = c
        far = {2: 2, -1: 1, 1: 1, 0: 0}[dp]
        return (stage, hop if stage == 0 else 0, far, hop, u, s)

    def link(c):
        return ((c[0] + c[1]) % 2, c[3])

    return simulate(todo, needs, rank, link, lambda c: 1.4 / c[4], 20)


HIST_RANK = (0, 0, 0, 0)
DEPTH = 10
TAIL = (4, 7, 9, 15, 27)
GATHER = plan_gather()
SPREAD = plan_spread()
RINGED = 2
PARTS = ((0, 112), (112, 48))
LEVELS = 256.0
TOP = 32767.0


def encode(values):
    most = jnp.maximum(jnp.max(jnp.abs(values), axis=0, keepdims=True), 1e-33)
    level = jnp.floor(jnp.log2(most) * LEVELS) + 2.0
    codes = jnp.round(values * (TOP * jnp.exp2(level * (-1.0 / LEVELS))))
    return codes.astype(jnp.int32).astype(jnp.int16), level


def level_rows(levels):
    row = lax.broadcasted_iota(jnp.int32, (16, levels[0].shape[1]), 0)
    tile = jnp.broadcast_to(levels[-1], row.shape)
    for i, level in enumerate(levels[:-1]):
        tile = jnp.where(row == i, level, tile)
    return tile.astype(jnp.int32).astype(jnp.int16)


def decode(codes, level):
    step = jnp.exp2(level * (1.0 / LEVELS)) * (1.0 / TOP)
    return codes.astype(jnp.int32).astype(jnp.float32) * step


def numbered(order):
    ids = {}
    for _, started in order:
        for c in started:
            ids[c] = len(ids)
    return ids


GATHER_IDS = numbered(GATHER)
SPREAD_IDS = numbered(SPREAD)


def kernel(
    planes, hist, mask, pairs, out,
    g_ref, h_ref, hp, acc, accp, r1, r2, r3, r4, dq, r5, pb, d_ref, e1, dt, e2,
    own_sem, hist_sem, send, recv, s1, v1, s2, v2, s3, v3, s4, v4, s5, v5, s6, v6,
    ts, tv, us, uv,
):
    cols, depth = planes.shape[1:]
    half, quarter = depth // 2, depth // 4
    rows = h_ref.shape[0]
    me = lax.axis_index("sess")
    z, x = me // RING, me % RING
    act = lax.axis_index("act")
    y, core = act // 2, act % 2
    place = (z, x)

    def wrap(v, d):
        return lax.rem(v + d + RING, RING)

    def near(axis, d):
        return {"sess": wrap(z, d) * RING + x if axis == 0 else z * RING + wrap(x, d)}

    def along_y(d):
        return {"act": wrap(y, d) * 2 + core}

    twin = {"act": y * 2 + 1 - core}

    def remote(src, dst, send_sem, recv_sem, device):
        return pltpu.make_async_remote_copy(
            src_ref=src, dst_ref=dst, send_sem=send_sem, recv_sem=recv_sem,
            device_id=device, device_id_type=MESH,
        )

    def toward(axis, way):
        even = 1 - 2 * lax.rem(place[axis] + core, 2)
        return even if way == MATE else -even

    def beside(axis, way):
        return near(axis, toward(axis, way))

    group = [lax.rem(place[k] - core + RING, RING) // 2 for k in (0, 1)]
    keep_at = [pl.multiple_of(k * half + group[k] * quarter, quarter) for k in (0, 1)]
    give_at = [pl.multiple_of(k * half + (1 - group[k]) * quarter, quarter) for k in (0, 1)]

    around = [(a, d) for a in (0, 1) for d in (1, -1)]
    peers = [near(a, d) | {"act": y * 2 + c} for a, d in around for c in (0, 1)]
    peers += [along_y(d) for d in (1, -1, 2)] + [twin]
    barrier = pltpu.get_barrier_semaphore()
    for peer in peers:
        pl.semaphore_signal(barrier, inc=1, device_id=peer, device_id_type=MESH)

    pieces = give_at + keep_at
    loads = []
    for i, at in enumerate(pieces):
        at = pl.ds(at, quarter)
        loads.append(pltpu.make_async_copy(hist.at[:, at], h_ref.at[:, at], hist_sem.at[i]))
        loads[i].start()
    owns = []
    for k in (0, 1):
        src = planes.at[:, :, pl.ds(keep_at[k], quarter)]
        owns.append(pltpu.make_async_copy(src, g_ref.at[:, k, me], own_sem.at[k]))
        owns[k].start()
    pl.semaphore_wait(barrier, len(peers))

    def mask_piece(i):
        loads[i].wait()
        first = pieces[i] // BLK

        def tile(j, _):
            at = pl.ds(pl.multiple_of(pieces[i] + j * BLK, BLK), BLK)
            for r in range(mask.shape[0]):
                keep = mask[r, first + j].astype(jnp.float32).astype(jnp.bfloat16)
                some = pl.ds(r * BLK, BLK)
                h_ref[some, at] = h_ref[some, at] * keep
            return 0

        lax.fori_loop(0, quarter // BLK, tile, 0)

    def ends(c):
        u, stage, dp, s, hop = c
        pc, qc = place[u % 2], place[1 - u % 2]
        axis = (u + stage) % 2
        if stage == 0:
            return pc if hop == 1 else wrap(pc, -s), qc, near(axis, s)
        return wrap(pc, dp), qc if hop == 1 else wrap(qc, -s), near(axis, s)

    def slot(c, p, q):
        return p * RING + q if c[0] % 2 == 0 else q * RING + p

    def gather_copy(c):
        u, stage, a, w, hop = c
        i = GATHER_IDS[c]
        g, k = u // 2, u % 2
        if stage == 2:
            some = pl.ds(a * BLK, BLK)
            src = h_ref.at[some, pl.ds(give_at[k], quarter)]
            return remote(src, hp.at[k, some], send.at[i], recv.at[i], beside(k, w))
        pc, qc = place[k], place[1 - k]
        axis = k if stage == 0 else 1 - k
        if stage == 0:
            p, q = wrap(pc, toward(k, PARTNER)) if a == 3 else pc, qc
        else:
            steps = (0, toward(k, PARTNER), toward(k, MATE), 2)
            p, q = wrap(pc, steps[a]), qc
            if hop == 2:
                q = wrap(qc, toward(1 - k, 1 - w))
        ref = g_ref.at[g, k, slot(c, p, q)]
        src = ref
        if hop == 2:
            ref = src = ref.at[:, pl.ds(w * quarter // 2, quarter // 2)]
        elif stage == 0 and a == 1:
            src = planes.at[g, :, pl.ds(give_at[k], quarter)]
        elif a == 0 or (stage == 0 and a == 2):
            src = planes.at[g, :, pl.ds(keep_at[k], quarter)]
        return remote(src, ref, send.at[i], recv.at[i], beside(axis, w))

    def spread_copy(h, c):
        p, q, device = ends(c)
        at = slot(c, p, q) * RING + 2 * c[0]
        if c[4] == 2:
            rows = pl.ds(at if c[3] == 1 else at + 1, 1)
        else:
            rows = pl.ds(at, 2)
        ref = pb.at[rows, pl.ds(*PARTS[h])]
        i = SPREAD_IDS[c]
        return remote(ref, ref, ts.at[h, i], tv.at[h, i], device)

    shape = (RING, 2, 2 * cols, rows)

    def multiply(g, k, first):
        some = g_ref[g, k].reshape(RING * RING * cols, quarter)
        dims = (((1,), (1,)), ((), ()))
        mine = h_ref[:, pl.ds(keep_at[k], quarter)]
        total = lax.dot_general(some, mine, dims, preferred_element_type=jnp.float32)
        total = total.reshape(shape)
        acc[g] = total if first else acc[g] + total

    def multiply_partner(g, k):
        some = g_ref[g, k].reshape(RING * RING * cols, quarter)
        dims = (((1,), (1,)), ((), ()))
        total = lax.dot_general(some, hp[k], dims, preferred_element_type=jnp.float32)
        if g < RINGED:
            accp[g, k] = total.reshape(shape)
        else:
            codes, level = encode(total)
            dq[g - RINGED, k, 0 : codes.shape[0]] = codes
            dq[g - RINGED, k, codes.shape[0] :] = level_rows([level])

    turn = {1: 0, -1: 1, 2: 2}

    def pair_copy(g):
        return remote(acc.at[g, :, 1 - core], r1.at[g], s1.at[g], v1.at[g], twin)

    def ring_copy(g, d):
        i = turn[d]
        src = acc.at[g, wrap(y, d), core]
        return remote(src, r2.at[g, i], s2.at[g, i], v2.at[g, i], along_y(d))

    def partner_ring(g, k, d):
        i = turn[d]
        src = accp.at[g, k, wrap(y, d)]
        return remote(src, r3.at[g, k, i], s4.at[g, k, i], v4.at[g, k, i], along_y(d))

    def home_copy(g, k, c):
        target = beside(k, PARTNER) | {"act": y * 2 + c}
        return remote(
            accp.at[g, k, y, c], r4.at[g, core, k], s5.at[g, k, c], v5.at[g, core, k], target
        )

    def home_wait(g, k, c):
        sem = v5.at[g, c, k]
        remote(r4.at[g, c, k], r4.at[g, c, k], s5.at[g, k, c], sem, twin).wait_recv()

    def direct_copy(g, k):
        i = g - RINGED
        return remote(dq.at[i, k], r5.at[i, k], s6.at[i, k], v6.at[i, k], beside(k, PARTNER))

    def reduce_first(g):
        if g >= RINGED:
            for k in (0, 1):
                direct_copy(g, k).wait_recv()
                many = RING * RING * cols
                level = r5[g - RINGED, k, many:].astype(jnp.int32).astype(jnp.float32)[0:1]
                acc[g] = acc[g] + decode(r5[g - RINGED, k, 0:many], level).reshape(shape)
        pair_copy(g).start()

    def reduce_second(g):
        pair_copy(g).wait_recv()
        acc[g, :, core] = acc[g, :, core] + r1[g]
        for d in (2, 1, -1):
            ring_copy(g, d).start()

    def reduce_partner(g):
        if g >= RINGED:
            return
        for k in (0, 1):
            for d in (1, -1, 2):
                partner_ring(g, k, d).wait_recv()
            accp[g, k, y] = accp[g, k, y] + r3[g, k, 0] + r3[g, k, 1] + r3[g, k, 2]
            for c in (0, 1):
                home_copy(g, k, c).start()

    def reduce_third(g):
        for d in (1, -1, 2):
            ring_copy(g, d).wait_recv()
        total = acc[g, y, core] + r2[g, 0] + r2[g, 1] + r2[g, 2]
        if g < RINGED:
            for k in (0, 1):
                for c in (0, 1):
                    home_wait(g, k, c)
                    total = total + r4[g, c, k]
        codes, level = encode(total)
        levels.append(level)
        last_of = g >= UNITS - 2
        at = g * 32 if g < UNITS - 1 else PARTS[1][0]
        tile = level_rows(levels[-1:] if g == UNITS - 1 else levels) if last_of else None
        for b in range(4):
            some = slice(b * BLK, (b + 1) * BLK)
            pb[me * RING + b, at : at + 32] = codes[:, some]
            if last_of:
                end = at + 32
                pb[me * RING + b, end : end + 16] = tile[:, some]

    levels = []

    def spread_steps(h, begin, end):
        for c, started in SPREAD[begin:end]:
            if c is not None:
                spread_copy(h, c).wait_recv()
            for c2 in started:
                spread_copy(h, c2).start()

    got = {u: 1.0 for u in range(2 * UNITS)}
    tiles = {0: 0, 1: 0}
    waiting, seen, later, held = [], set(), [], []
    steps = len(SPREAD)
    last = max(n for n, (_, started) in enumerate(GATHER) if started)
    for n, (c, started) in enumerate(GATHER):
        if c == MASKED:
            mask_piece(0)
            mask_piece(1)
        elif c is not None:
            gather_copy(c).wait_recv()
            if c[1] == 2:
                tiles[c[0]] += 1
            else:
                got[c[0]] += 1.0 / c[4]
                if got[c[0]] == 16.0:
                    waiting.append(c[0])
        for c2 in started:
            gather_copy(c2).start()
        if c == MASKED:
            mask_piece(2)
            mask_piece(3)
            owns[0].wait()
            owns[1].wait()
        for due, do in [e for e in later if e[0] <= n]:
            do()
        later = [e for e in later if e[0] > n]
        if n == last:
            assert not later, later
            spread_steps(0, 0, 1)
        for u in [u for u in waiting if tiles[u % 2] == 4]:
            waiting.remove(u)
            g, k = u // 2, u % 2
            multiply_partner(g, k)
            if g >= RINGED:
                direct_copy(g, k).start()
            else:
                for d in (2, 1, -1):
                    partner_ring(g, k, d).start()
            if g == UNITS - 1:
                held.append(k)
                continue
            multiply(g, k, g not in seen)
            if g in seen and g >= RINGED:
                later.append((n + 10, lambda g=g: reduce_first(g)))
                later.append((n + 15, lambda g=g: reduce_second(g)))
                later.append((n + 21, lambda g=g: reduce_third(g)))
            elif g in seen:
                reduce_first(g)
                later.append((n + 4, lambda g=g: reduce_second(g)))
                later.append((n + WAIT_PARTNER, lambda g=g: reduce_partner(g)))
                later.append((n + WAIT_HOME, lambda g=g: reduce_third(g)))
            seen.add(g)

    assert not waiting and not later and len(held) == 2
    g = UNITS - 1
    spread_steps(0, 1, TAIL[0])
    multiply(g, held[0], True)
    spread_steps(0, TAIL[0], TAIL[1])
    multiply(g, held[1], False)
    spread_steps(0, TAIL[1], TAIL[2])
    reduce_first(g)
    spread_steps(0, TAIL[2], TAIL[3])
    reduce_second(g)
    spread_steps(0, TAIL[3], TAIL[4])
    reduce_third(g)
    spread_steps(1, 0, 1)
    spread_steps(0, TAIL[4], steps)
    spread_steps(1, 1, steps)

    def one_pair(c, i):
        k = 4 * (i // 2) + 2 * c + i % 2

        def block(i):
            level = pb[i, 96:112].astype(jnp.int32).astype(jnp.float32)
            out = [decode(pb[i, g * 32 : (g + 1) * 32], level[g : g + 1]) for g in range(3)]
            level = pb[i, 144:160].astype(jnp.int32).astype(jnp.float32)
            out.append(decode(pb[i, 112:144], level[0:1]))
            return jnp.concatenate(out, axis=0)

        lt = block(pairs[k, 0])
        rt = block(pairs[k, 1])
        dots = lax.dot_general(
            lt, rt, (((0,), (0,)), ((), ())),
            precision=lax.Precision.HIGHEST, preferred_element_type=jnp.float32,
        )
        at = d_ref.at[c, i // 2, i % 2]
        at[0:BLK] = dots
        at[BLK : BLK + 8] = jnp.broadcast_to(jnp.sum(lt * lt, axis=0, keepdims=True), (8, BLK))
        at[BLK + 8 : BLK + 16] = jnp.broadcast_to(jnp.sum(rt * rt, axis=0, keepdims=True), (8, BLK))
        return 0

    def pairs_of(c):
        return lax.fori_loop(0, pairs.shape[0] // 2, lambda i, _: one_pair(c, i), 0, unroll=8)

    pairs_of(1 - core)
    swap = remote(d_ref.at[1 - core], e1, s3, v3, twin)
    swap.start()
    pairs_of(core)
    swap.wait_recv()

    def share_copy(d):
        i = turn[d]
        return remote(dt.at[i], e2.at[i], us.at[i], uv.at[i], along_y(d))

    for d in (2, 1, -1):
        i, there = turn[d], wrap(y, d)
        for j in range(2):
            total = d_ref[core, there, j] + e1[there, j]
            codes, level = encode(total[0:BLK])
            square_codes, square_level = encode(total[BLK:])
            dt[i, j, 0:BLK] = codes
            dt[i, j, BLK : BLK + 16] = square_codes
            dt[i, j, BLK + 16 :] = level_rows([level, square_level])
        share_copy(d).start()
    totals = [d_ref[core, y, j] + e1[y, j] for j in range(2)]
    dots = [t[0:BLK] for t in totals]
    squares = [t[BLK:] for t in totals]
    for d in (1, -1, 2):
        i = turn[d]
        share_copy(d).wait_recv()
        for j in range(2):
            level = e2[i, j, BLK + 16 :].astype(jnp.int32).astype(jnp.float32)
            dots[j] = dots[j] + decode(e2[i, j, 0:BLK], level[0:1])
            squares[j] = squares[j] + decode(e2[i, j, BLK : BLK + 16], level[1:2])
    for j in range(2):
        lscale = lax.rsqrt(squares[j][0:1] / P_SIZE + 1e-06)
        rscale = lax.rsqrt(squares[j][8:9] / P_SIZE + 1e-06)
        lfull = jnp.broadcast_to(lscale, (BLK, BLK)).T
        out[j] = dots[j] / P_SIZE * lfull * rscale

    for c in GATHER_IDS:
        gather_copy(c).wait_send()
    for h in range(2):
        for c in SPREAD_IDS:
            spread_copy(h, c).wait_send()
    for g in range(UNITS):
        pair_copy(g).wait_send()
        for d in (1, -1, 2):
            ring_copy(g, d).wait_send()
        for k in (0, 1):
            if g >= RINGED:
                direct_copy(g, k).wait_send()
                continue
            for d in (1, -1, 2):
                partner_ring(g, k, d).wait_send()
            for c in (0, 1):
                home_copy(g, k, c).wait_send()
    swap.wait_send()
    for d in (1, -1, 2):
        share_copy(d).wait_send()


def body(hist, tile_mask, planes, pairs):
    rows, depth = hist.shape
    cols = planes.shape[1] // UNITS
    f32 = jnp.float32
    dma = pltpu.SemaphoreType.DMA
    return pl.pallas_call(
        kernel,
        out_shape=jax.ShapeDtypeStruct((2, BLK, BLK), f32),
        in_specs=[
            pl.BlockSpec(memory_space=pl.ANY),
            pl.BlockSpec(memory_space=pl.ANY),
            pl.BlockSpec(memory_space=pltpu.SMEM),
            pl.BlockSpec(memory_space=pltpu.SMEM),
        ],
        out_specs=pl.BlockSpec(memory_space=pltpu.VMEM),
        scratch_shapes=[
            pltpu.VMEM((UNITS, 2, RING * RING, cols, depth // 4), jnp.bfloat16),
            pltpu.VMEM((rows, depth), jnp.bfloat16),
            pltpu.VMEM((2, rows, depth // 4), jnp.bfloat16),
            pltpu.VMEM((UNITS, RING, 2, 2 * cols, rows), f32),
            pltpu.VMEM((RINGED, 2, RING, 2, 2 * cols, rows), f32),
            pltpu.VMEM((UNITS, RING, 2 * cols, rows), f32),
            pltpu.VMEM((UNITS, 3, 2 * cols, rows), f32),
            pltpu.VMEM((RINGED, 2, 3, 2, 2 * cols, rows), f32),
            pltpu.VMEM((RINGED, 2, 2, 2 * cols, rows), f32),
            pltpu.VMEM((UNITS - RINGED, 2, RING * RING * cols + 16, rows), jnp.int16),
            pltpu.VMEM((UNITS - RINGED, 2, RING * RING * cols + 16, rows), jnp.int16),
            pltpu.VMEM((RING * RING * RING, 160, BLK), jnp.int16),
            pltpu.VMEM((2, RING, 2, BLK + 16, BLK), f32),
            pltpu.VMEM((RING, 2, BLK + 16, BLK), f32),
            pltpu.VMEM((3, 2, BLK + 32, BLK), jnp.int16),
            pltpu.VMEM((3, 2, BLK + 32, BLK), jnp.int16),
            dma((2,)),
            dma((4,)),
            dma((len(GATHER_IDS),)),
            dma((len(GATHER_IDS),)),
            dma((UNITS,)),
            dma((UNITS,)),
            dma((UNITS, 3)),
            dma((UNITS, 3)),
            dma,
            dma,
            dma((RINGED, 2, 3)),
            dma((RINGED, 2, 3)),
            dma((RINGED, 2, 2)),
            dma((RINGED, 2, 2)),
            dma((UNITS - RINGED, 2)),
            dma((UNITS - RINGED, 2)),
            dma((2, len(SPREAD_IDS))),
            dma((2, len(SPREAD_IDS))),
            dma((3,)),
            dma((3,)),
        ],
        compiler_params=pltpu.CompilerParams(
            collective_id=0, has_side_effects=True, vmem_limit_bytes=63 * 2**20
        ),
    )(planes.T.reshape(UNITS, cols, depth), hist, tile_mask, pairs)


def solution(mesh):
    placed = (P("sess", "act"), P("sess", "act"), P("act", "sess"), P("sess", None))
    return jax.shard_map(
        body, mesh=mesh, in_specs=placed, out_specs=P(("sess", "act"), None, None), check_vma=False
    )
```
